256 devices in a mesh: blk: 64 (over x_hi, z, y), tp: 4 (over x_lo, core).
Axes of the slice: x: 4 (x_hi: 2, x_lo: 2; x = x_hi * 2 + x_lo), y: 4, z: 8, core: 2. Of those that a mesh axis runs over, the one named last changes fastest.
Arguments:
- text_query: bfloat16 [8192, 4096], P('blk', 'tp'), may hold values from -4.5 to 4.5
- text_keyval: bfloat16 [2, 8192, 4096], P(None, 'blk', 'tp'), may hold values from -4.5 to 4.5
- frame_features: bfloat16 [16384, 1024], P(('blk', 'tp')), may hold values from -6 to 6
- frame_proj: bfloat16 [1024, 3, 4096], P(None, None, 'tp'), may hold values from -0.1875 to 0.1875
- frame_slot: int32 [64, 4], P('blk'), may hold values from 0 to 3, each once within a row
- counts: int32 [64, 2], replicated, may hold values from 0 to 128, as said below
- block_mask: int32 [64, 4], P('blk'), may hold values from 0 to 1, as said below
Outputs:
- attended: bfloat16 [24576, 4096], P('blk', 'tp')
The draws below stay inside these ranges and needn't reach their ends.
Inputs may be any that keep to these rules, and one draw needn't show every extreme that they name: `frame_slot`: each row is an ordering of the block's 4 encoded frames. `counts`: row b holds block b's live frames (0 to 4) and live text tokens (2 to 128); in every draw some block has 4 live frames, some has none, and some has 128 live text tokens. `block_mask`: column 0 is all ones; entry [c, d] is 0 where d > c; some row is all ones.
All inputs are finite; a program needn't handle non-finite values.
Results may differ from the reference program's by a relative error of at most 0.0065.
Values may be sent and summed in bfloat16 or wider, within the bound.
No kernel may reach another device: no remote copies, remote signals or barrier semaphores. Data moves between devices by JAX's collectives and lax.ppermute only.
A program may use at most 64 MiB of HBM per device.

```python
import math
import jax
import jax.numpy as jnp
from jax import lax

HEADS = 32
HD = 128
VW = 1024
FT = 64
REACH = 4
TEXT_CAP = 128
FRAME_CAP = 4
FRAME_ROWS = 16384
N_BLK = 64


def draw_text_query(key, part):
    shape = (N_BLK, TEXT_CAP, HEADS * HD)
    own_key = jax.random.fold_in(key, 1)
    values = jnp.clip(jax.random.normal(own_key, shape, jnp.float32), -4.5, 4.5)
    return values.reshape(N_BLK * TEXT_CAP, HEADS * HD).astype(jnp.bfloat16)


def draw_text_keyval(key, part):
    shape = (2, N_BLK, TEXT_CAP, HEADS * HD)
    own_key = jax.random.fold_in(key, 2)
    values = jnp.clip(jax.random.normal(own_key, shape, jnp.float32), -4.5, 4.5)
    return values.reshape(2, N_BLK * TEXT_CAP, HEADS * HD).astype(jnp.bfloat16)


def draw_counts(key, part):
    frames = jax.random.randint(jax.random.fold_in(key, 3), (N_BLK,), 0, FRAME_CAP + 1)
    texts = jax.random.randint(jax.random.fold_in(key, 4), (N_BLK,), 2, TEXT_CAP + 1)
    ordering = jax.random.permutation(jax.random.fold_in(key, 5), N_BLK)
    frames = frames.at[ordering[0]].set(FRAME_CAP).at[ordering[1]].set(0)
    texts = texts.at[ordering[2]].set(TEXT_CAP)
    return jnp.stack([frames, texts], axis=1).astype(jnp.int32)


def draw_block_mask(key, part):
    rows = jnp.arange(N_BLK)[:, None]
    distance = jnp.arange(REACH)[None, :]
    coins = jax.random.randint(jax.random.fold_in(key, 6), (N_BLK, REACH), 0, 2)
    full_row = jax.random.randint(jax.random.fold_in(key, 7), (), REACH - 1, N_BLK)
    picked = jnp.where(rows == full_row, 1, coins)
    picked = jnp.where(distance == 0, 1, picked)
    return jnp.where(rows >= distance, picked, 0).astype(jnp.int32)


def block_scale(stream_key, shape, cuts, smallest, top_value):
    gain, own = 1.0, jax.random.fold_in(stream_key, 6)
    for axis_at, shards_of in cuts:
        heights = jnp.exp(jax.random.uniform(jax.random.fold_in(own, axis_at), (shards_of,), jnp.float32, smallest / len(cuts), top_value / len(cuts)))
        gain = gain * jnp.repeat(heights, shape[axis_at] // shards_of).reshape([-1 if axis == axis_at else 1 for axis in range(len(shape))])
    return gain


def noise(key, dims, deviation, bound, split=(), kind=jnp.bfloat16):
    values = deviation * jax.random.normal(key, dims, jnp.float32)
    if split:
        values = values * block_scale(key, dims, split, -0.22, 0.18)
    return jnp.clip(values, -bound, bound).astype(kind)


def setup_inputs(seed: int = 0) -> dict:
    splits = jax.random.split(jax.random.key(seed), 8)
    return {
        "text_query": draw_text_query(jax.random.fold_in(splits[7], 71), 0),
        "text_keyval": draw_text_keyval(jax.random.fold_in(splits[7], 71), 0),
        "frame_features": noise(splits[2], (FRAME_ROWS, VW), 1.0, 6.0, ((0, 256),)),
        "frame_proj": noise(splits[3], (VW, 3, HEADS * HD), VW ** -0.5, 0.1875, ((2, 4),)),
        "frame_slot": jax.vmap(lambda own: jax.random.permutation(own, FRAME_CAP))(jax.random.split(splits[4], N_BLK)).reshape((N_BLK, FRAME_CAP)).astype(jnp.int32),
        "counts": draw_counts(jax.random.fold_in(splits[7], 71), 0),
        "block_mask": draw_block_mask(jax.random.fold_in(splits[7], 71), 0),
    }


def live_slots(count_row, frame_rows, text_cap):
    slots = jnp.arange(frame_rows + text_cap, dtype=jnp.int32)
    frame_live = (slots < frame_rows) & (slots // FT < count_row[0])
    text_live = (slots >= frame_rows) & (slots - frame_rows < count_row[1])
    return frame_live | text_live

def block_partial(queries, pair, allowed):
    heads = queries.shape[1]
    span = pair.shape[1]
    keys = pair[0].reshape(span, heads, HD).astype(jnp.float32)
    values = pair[1].reshape(span, heads, HD).astype(jnp.float32)
    scores = jnp.einsum('qhd,khd->hqk', queries.astype(jnp.float32), keys) * (1.0 / math.sqrt(HD))
    scores = jnp.where(allowed[None], scores, -1e+30)
    row_max = lax.optimization_barrier(jnp.max(scores, axis=2))
    expo = jnp.exp(scores - row_max[:, :, None])
    normalizer = lax.optimization_barrier(jnp.sum(expo, axis=2))
    weights = lax.optimization_barrier(expo.astype(jnp.bfloat16))
    weighted = jnp.einsum('hqk,khd->hqd', weights.astype(jnp.float32), values)
    return (row_max, weighted, normalizer)

def absorb(running, incoming):
    old_max, old_weighted, old_norm = running
    new_max, new_weighted, new_norm = incoming
    joint = jnp.maximum(old_max, new_max)
    keep_old = jnp.exp(old_max - joint)
    keep_new = jnp.exp(new_max - joint)
    weighted = old_weighted * keep_old[:, :, None] + new_weighted * keep_new[:, :, None]
    return (joint, weighted, old_norm * keep_old + new_norm * keep_new)

def reference(text_query, text_keyval, frame_features, frame_proj, frame_slot, counts, block_mask):
    width = HEADS * HD
    frame_rows = FRAME_CAP * FT
    span = frame_rows + TEXT_CAP
    feats = frame_features.astype(jnp.float32)
    normed = feats * lax.rsqrt(lax.optimization_barrier(jnp.mean(feats * feats, axis=1, keepdims=True)) + 1e-05)
    projected = jnp.dot(normed.astype(jnp.bfloat16), frame_proj.reshape(VW, 3 * width), preferred_element_type=jnp.float32).astype(jnp.bfloat16)
    projected = lax.optimization_barrier(projected)
    projected = projected.reshape(N_BLK, FRAME_CAP, FT, 3, width)
    placed = jax.vmap(lambda frames, ordering: jnp.take(frames, ordering, axis=0))(projected, frame_slot)
    placed = placed.reshape(N_BLK, frame_rows, 3, width)
    text_rows = text_query.reshape(N_BLK, TEXT_CAP, width)
    text_pairs = text_keyval.reshape(2, N_BLK, TEXT_CAP, width)
    queries = jnp.concatenate([placed[:, :, 0], text_rows], axis=1)
    key_rows = jnp.concatenate([placed[:, :, 1], text_pairs[0]], axis=1)
    value_rows = jnp.concatenate([placed[:, :, 2], text_pairs[1]], axis=1)
    pairs = jnp.stack([key_rows, value_rows], axis=1)
    slots = jnp.arange(span, dtype=jnp.int32)
    causal = slots[:, None] >= slots[None, :]

    def one_block(block_index):
        own_queries = queries[block_index].reshape(span, HEADS, HD)
        query_live = live_slots(counts[block_index], frame_rows, TEXT_CAP)
        running = block_partial(own_queries, pairs[block_index], query_live[None, :] & causal)
        for distance in range(1, REACH):
            source = jnp.maximum(block_index - distance, 0).astype(jnp.int32)
            key_live = live_slots(counts[source], frame_rows, TEXT_CAP)
            incoming = block_partial(own_queries, pairs[source], jnp.broadcast_to(key_live[None, :], (span, span)))
            merged = absorb(running, incoming)
            flag = block_mask[block_index, distance] > 0
            running = jax.tree.map(lambda previous, combined: jnp.where(flag, combined, previous), running, merged)
        row_max, weighted, normalizer = running
        result = weighted / normalizer[:, :, None]
        result = jnp.transpose(result, (1, 0, 2)).reshape(span, width)
        return jnp.where(query_live[:, None], result, 0.0).astype(jnp.bfloat16)
    outputs = lax.map(one_block, jnp.arange(N_BLK, dtype=jnp.int32))
    return outputs.reshape(N_BLK * span, width)
```

```python
import math

import jax
import jax.numpy as jnp
from jax import lax
from jax.experimental import pallas as pl
from jax.experimental.pallas import tpu as pltpu
from jax.sharding import PartitionSpec as P

HD = 128
FT = 64
REACH = 4
PAD = 16
ROWS = FT + PAD
LOG2E = 1.4426950408889634
NEG = -1e30
VM = pl.BlockSpec(memory_space=pltpu.VMEM)
SM = pl.BlockSpec(memory_space=pltpu.SMEM)
ANY = pl.BlockSpec(memory_space=pl.ANY)
F32 = jnp.float32
BF16 = jnp.bfloat16


def dot_nt(a, b):
    return lax.dot_general(a, b, (((1,), (1,)), ((), ())), preferred_element_type=F32)


def dot_nn(a, b):
    return lax.dot_general(a, b, (((1,), (0,)), ((), ())), preferred_element_type=F32)


def prep_kernel(slot_ref, feat_ref, out_ref):
    me = lax.axis_index("tp")
    slot = jnp.int32(0)
    for j in range(1, slot_ref.shape[1]):
        slot = jnp.where(slot_ref[0, j] == me, jnp.int32(j), slot)
    feats = feat_ref[...].astype(F32)
    normed = feats * lax.rsqrt(jnp.mean(feats * feats, axis=1, keepdims=True) + 1e-05)
    out_ref[:FT, :] = normed.astype(BF16)
    out_ref[FT:, :] = jnp.full((PAD, out_ref.shape[1]), slot.astype(F32), F32).astype(BF16)


def slot_of(payload):
    return jnp.max(payload[FT:ROWS, :128].astype(F32)).astype(jnp.int32)


def soft_step(s, values, ones):
    top = jnp.max(s, axis=1, keepdims=True)
    p = jnp.exp2(s - top).astype(BF16)
    return top, dot_nn(p, jnp.concatenate([values, ones], axis=1))


def own_kernel(
    counts_ref, pay0, payx, payc, tq, tkv, w_hbm, q_out, acc_out, m_out, l_out, x, kbuf, vbuf, wbuf, sems
):
    width = tq.shape[1]
    heads = width // HD
    half = width // 2
    b = lax.axis_index("blk")
    copies = []
    for m in range(3):
        for n in range(2):
            c = pltpu.make_async_copy(
                w_hbm.at[m, :, pl.ds(n * half, half)], wbuf.at[m, :, pl.ds(n * half, half)], sems.at[2 * m + n]
            )
            c.start()
            copies.append(c)
    for pay in (pay0[...], payx[...], payc[0], payc[1]):
        at = pl.multiple_of(slot_of(pay) * FT, FT)
        x[pl.ds(at, FT), :] = pay[:FT]
    q_out[256:, :] = tq[...]
    kbuf[256:, :] = tkv[0]
    vbuf[256:, :] = tkv[1]
    rows = x[...]
    for m, out in enumerate((q_out, kbuf, vbuf)):
        for n in range(2):
            copies[2 * m + n].wait()
            out[:256, n * half : (n + 1) * half] = dot_nn(rows, wbuf[m, :, n * half : (n + 1) * half]).astype(BF16)
    nf = counts_ref[0, b]
    nt = counts_ref[1, b]
    ones = jnp.ones((384, HD), BF16)
    scale = LOG2E / math.sqrt(HD)
    for tile in range(3):
        span = (tile + 1) * 128
        qpos = lax.broadcasted_iota(jnp.int32, (128, span), 0) + tile * 128
        kpos = lax.broadcasted_iota(jnp.int32, (128, span), 1)
        live = (kpos < nf * FT) | ((kpos >= 256) & (kpos - 256 < nt))
        bias = jnp.where(live & (qpos >= kpos), 0.0, NEG)
        lane = lax.broadcasted_iota(jnp.int32, (128, 128), 1)
        m_all = jnp.zeros((128, 128), F32)
        l_all = jnp.zeros((128, 128), F32)
        for h in range(heads):
            cols = slice(h * HD, (h + 1) * HD)
            s = dot_nt(q_out[tile * 128 : span, cols], kbuf[:span, cols]) * scale + bias
            top, o = soft_step(s, vbuf[:span, cols], ones[:span])
            acc_out[tile * 128 : span, cols] = o[:, :HD]
            m_all = jnp.where(lane == h, top, m_all)
            l_all = jnp.where(lane == h, o[:, HD:], l_all)
        m_out[tile * 128 : span, :] = m_all
        l_out[tile * 128 : span, :] = l_all


def merge(q, keys, values, bias, acc, m_old, l_old, ones, scale):
    s = dot_nt(q, keys) * scale + bias
    top = jnp.maximum(jnp.max(s, axis=1, keepdims=True), m_old)
    p = jnp.exp2(s - top).astype(BF16)
    o = dot_nn(p, jnp.concatenate([values, ones], axis=1))
    keep = jnp.exp2(m_old - top)
    return top, acc * keep + o[:, :HD], l_old * keep + o[:, HD:]


def frames_kernel(
    counts_ref, mask_ref, p1, p3, p13x, p13c, p2, p2x, p2c, q, w_hbm, acc_in, m_in, l_in, acc, m_out, l_out,
    x, kbuf, vbuf, wbuf, sems
):
    width = q.shape[1]
    heads = width // HD
    b = lax.axis_index("blk")
    copies = []
    for m in range(2):
        c = pltpu.make_async_copy(w_hbm.at[m + 1], wbuf.at[m], sems.at[m])
        c.start()
        copies.append(c)
    acc[...] = acc_in[...]
    m_out[...] = m_in[...]
    l_out[...] = l_in[...]
    for c in copies:
        c.wait()
    ones = jnp.ones((256, HD), BF16)
    scale = LOG2E / math.sqrt(HD)
    groups = {
        1: (lambda: p1[...], lambda: p13x[0], lambda: p13c[0], lambda: p13c[2]),
        2: (lambda: p2[...], lambda: p2x[...], lambda: p2c[0], lambda: p2c[1]),
        3: (lambda: p3[...], lambda: p13x[1], lambda: p13c[1], lambda: p13c[3]),
    }
    for d in (1, 3, 2):
        nf = counts_ref[0, jnp.maximum(b - d, 0)]

        @pl.when((mask_ref[0, d] > 0) & (nf > 0))
        def _(d=d, nf=nf):
            bias = jnp.zeros((1, 256), F32)
            col = lax.broadcasted_iota(jnp.int32, (1, 256), 1) // FT
            for j, get in enumerate(groups[d]):
                pay = get()
                x[j * FT : (j + 1) * FT, :] = pay[:FT]
                bias = jnp.where((col == j) & (slot_of(pay) >= nf), NEG, bias)
            rows = x[...]
            kbuf[...] = dot_nn(rows, wbuf[0]).astype(BF16)
            vbuf[...] = dot_nn(rows, wbuf[1]).astype(BF16)
            lane = lax.broadcasted_iota(jnp.int32, (384, 128), 1)
            m_all = m_out[...]
            l_all = l_out[...]
            for h in range(heads):
                cols = slice(h * HD, (h + 1) * HD)
                top, a, l = merge(
                    q[:, cols], kbuf[:, cols], vbuf[:, cols], bias, acc[:, cols],
                    m_all[:, h : h + 1], l_all[:, h : h + 1], ones, scale,
                )
                acc[:, cols] = a
                m_all = jnp.where(lane == h, top, m_all)
                l_all = jnp.where(lane == h, l, l_all)
            m_out[...] = m_all
            l_out[...] = l_all


def text_kernel(counts_ref, mask_ref, t1, t2, t3, q, acc, m_in, l_in, out):
    width = q.shape[1]
    heads = width // HD
    b = lax.axis_index("blk")
    scale = LOG2E / math.sqrt(HD)
    ones = jnp.ones((384, HD), BF16)
    biases = []
    for d in (1, 2, 3):
        nt = counts_ref[1, jnp.maximum(b - d, 0)]
        nt = jnp.where(mask_ref[0, d] > 0, nt, 0)
        col = lax.broadcasted_iota(jnp.int32, (1, 128), 1)
        biases.append(jnp.where(col < nt, 0.0, NEG))
    bias = jnp.concatenate(biases, axis=1)
    nf = counts_ref[0, b]
    nt = counts_ref[1, b]
    row = lax.broadcasted_iota(jnp.int32, (384, HD), 0)
    live = (row < nf * FT) | ((row >= 256) & (row - 256 < nt))
    m_all = m_in[...]
    l_all = l_in[...]
    for h in range(heads):
        cols = slice(h * HD, (h + 1) * HD)
        keys = jnp.concatenate([t[0, :, cols] for t in (t1, t2, t3)], axis=0)
        values = jnp.concatenate([t[1, :, cols] for t in (t1, t2, t3)], axis=0)
        _, a, l = merge(
            q[:, cols], keys, values, bias, acc[:, cols], m_all[:, h : h + 1], l_all[:, h : h + 1], ones, scale
        )
        out[:, cols] = jnp.where(live, a / l, 0.0).astype(BF16)


def shift(value, by, wrap=()):
    length = lax.axis_size("blk")
    pairs = [(i, i + by) for i in range(length) if 0 <= i + by < length]
    pairs += [(i, (i + by) % length) for i in wrap]
    return lax.ppermute(value, "blk", pairs)


def across(value, bit):
    return lax.ppermute(value, "tp", [(i, i ^ bit) for i in range(lax.axis_size("tp"))])


def body(text_query, text_keyval, frame_features, frame_proj, frame_slot, counts, block_mask):
    width = text_query.shape[1]
    span = 384
    vw = frame_features.shape[1]
    weights = jnp.transpose(frame_proj, (1, 0, 2))
    counts = counts.T
    n_blk = lax.axis_size("blk")
    pay = pl.pallas_call(
        prep_kernel,
        out_shape=jax.ShapeDtypeStruct((ROWS, vw), BF16),
        in_specs=[SM, VM],
        out_specs=VM,
        name="prep",
    )(frame_slot, frame_features)
    own_x = across(pay, 2)
    own_c = across(jnp.stack([pay, own_x]), 1)
    p1 = shift(pay, 1)
    p3 = shift(pay, 3)
    p2 = shift(pay, 2)
    t1 = shift(text_keyval, 1)
    t3 = shift(text_keyval, 3, wrap=(n_blk - 3,))
    p13x = across(jnp.stack([p1, p3]), 2)
    p13c = across(jnp.concatenate([jnp.stack([p1, p3]), p13x]), 1)
    p2x = across(p2, 2)
    p2c = across(jnp.stack([p2, p2x]), 1)
    t2 = shift(t3, -1, wrap=(0,))
    f32s = jax.ShapeDtypeStruct((span, width), F32)
    stat = jax.ShapeDtypeStruct((span, 128), F32)
    q, acc, m, l = pl.pallas_call(
        own_kernel,
        out_shape=(jax.ShapeDtypeStruct((span, width), BF16), f32s, stat, stat),
        in_specs=[SM, VM, VM, VM, VM, VM, ANY],
        out_specs=(VM,) * 4,
        scratch_shapes=[
            pltpu.VMEM((256, vw), BF16),
            pltpu.VMEM((span, width), BF16),
            pltpu.VMEM((span, width), BF16),
            pltpu.VMEM((3, vw, width), BF16),
            pltpu.SemaphoreType.DMA((6,)),
        ],
        cost_estimate=pl.CostEstimate(flops=3_000_000_000, transcendentals=1_000_000, bytes_accessed=8_000_000),
        name="own",
    )(counts, pay, own_x, own_c, text_query, text_keyval, weights)
    acc, m, l = pl.pallas_call(
        frames_kernel,
        out_shape=(f32s, stat, stat),
        in_specs=[SM, SM] + [VM] * 8 + [ANY] + [VM] * 3,
        out_specs=(VM,) * 3,
        scratch_shapes=[
            pltpu.VMEM((256, vw), BF16),
            pltpu.VMEM((256, width), BF16),
            pltpu.VMEM((256, width), BF16),
            pltpu.VMEM((2, vw, width), BF16),
            pltpu.SemaphoreType.DMA((2,)),
        ],
        cost_estimate=pl.CostEstimate(flops=5_000_000_000, transcendentals=2_000_000, bytes_accessed=8_000_000),
        name="frames",
    )(counts, block_mask, p1, p3, p13x, p13c, p2, p2x, p2c, q, weights, acc, m, l)
    return pl.pallas_call(
        text_kernel,
        out_shape=jax.ShapeDtypeStruct((span, width), BF16),
        in_specs=[SM, SM] + [VM] * 7,
        out_specs=VM,
        cost_estimate=pl.CostEstimate(flops=1_000_000_000, transcendentals=1_000_000, bytes_accessed=4_000_000),
        name="text",
    )(counts, block_mask, t1, t2, t3, q, acc, m, l)


def solution(mesh):
    placed = (
        P("blk", "tp"),
        P(None, "blk", "tp"),
        P(("blk", "tp"), None),
        P(None, None, "tp"),
        P("blk", None),
        P(),
        P("blk", None),
    )
    return jax.shard_map(
        body, mesh=mesh, in_specs=placed, out_specs=P("blk", "tp"), check_vma=False
    )
```

```python
import math

import jax
import jax.numpy as jnp
from jax import lax
from jax.experimental import pallas as pl
from jax.experimental.pallas import tpu as pltpu
from jax.sharding import PartitionSpec as P

HD = 128
FT = 64
REACH = 4
PAD = 8
ROWS = FT + PAD
NEG = -1e30
SCALE = 1.4426950408889634 / math.sqrt(HD)
LOW, HIGH = 2.0**-60, 2.0**100
VM = pl.BlockSpec(memory_space=pltpu.VMEM)
SM = pl.BlockSpec(memory_space=pltpu.SMEM)
F32 = jnp.float32
BF16 = jnp.bfloat16
PARAMS = pltpu.CompilerParams(vmem_limit_bytes=24 << 20)


def dot_nt(a, b):
    return lax.dot_general(a, b, (((1,), (1,)), ((), ())), preferred_element_type=F32)


def dot_nn(a, b):
    return lax.dot_general(a, b, (((1,), (0,)), ((), ())), preferred_element_type=F32)


def prep_kernel(slot_ref, feat_ref, out_ref):
    me = lax.axis_index("tp")
    slot = jnp.int32(0)
    for j in range(1, slot_ref.shape[1]):
        slot = jnp.where(slot_ref[0, j] == me, jnp.int32(j), slot)
    feats = feat_ref[...].astype(F32)
    normed = feats * lax.rsqrt(jnp.mean(feats * feats, axis=1, keepdims=True) + 1e-05)
    out_ref[:FT, :] = normed.astype(BF16)
    out_ref[FT:, :] = jnp.full((PAD, out_ref.shape[1]), slot.astype(F32), F32).astype(BF16)


def slot_of(pay):
    return jnp.max(pay[FT:ROWS, :128].astype(F32)).astype(jnp.int32)


def live_rows(shape, nf, nt, frames):
    row = lax.broadcasted_iota(jnp.int32, shape, 0)
    return (row < nf * FT) | ((row >= frames) & (row - frames < nt))


def key_block(counts_ref, mask_ref, d, which):
    b = lax.axis_index("blk")
    return jnp.where(mask_ref[0, d] > 0, counts_ref[which, jnp.maximum(b - d, 0)], 0)


def own_kernel(counts_ref, pay0, payx, payc, tq, tkv, w, q_out, acc, l_out, x, kbuf, vbuf):
    cap, width = tq.shape
    frames = x.shape[0]
    span = frames + cap
    b = lax.axis_index("blk")
    nf = counts_ref[0, b]
    nt = counts_ref[1, b]
    for pay in (pay0[...], payx[...], payc[0], payc[1]):
        x[pl.ds(pl.multiple_of(slot_of(pay) * FT, FT), FT), :] = pay[:FT]
    q_out[frames:, :] = tq[...]
    kbuf[frames:, :] = tkv[0]
    trow = lax.broadcasted_iota(jnp.int32, (cap, width), 0)
    vbuf[frames:, :] = jnp.where(trow < nt, tkv[1], jnp.zeros_like(tkv[1]))
    rows = x[...]
    half = width // 2
    frow = lax.broadcasted_iota(jnp.int32, (frames, half), 0)
    for n in range(2):
        c = slice(n * half, (n + 1) * half)
        q_out[:frames, c] = dot_nn(rows, w[0, :, c]).astype(BF16)
        kbuf[:frames, c] = dot_nn(rows, w[1, :, c]).astype(BF16)
        vbuf[:frames, c] = jnp.where(frow < nf * FT, dot_nn(rows, w[2, :, c]), 0.0).astype(BF16)
    ones = jnp.where(live_rows((span, HD), nf, nt, frames), 1.0, 0.0).astype(BF16)
    step = cap
    causal = lax.broadcasted_iota(jnp.int32, (step, step), 0) >= lax.broadcasted_iota(jnp.int32, (step, step), 1)
    for h in range(width // HD):
        cols = slice(h * HD, (h + 1) * HD)
        for lo in range(0, span, step):
            hi = lo + step
            p = jnp.exp2(dot_nt(q_out[lo:hi, cols], kbuf[:hi, cols]) * SCALE)
            diag = jnp.where(causal, p[:, lo:hi], 0.0)
            p = jnp.concatenate([p[:, :lo], diag], axis=1) if lo else diag
            o = dot_nn(p.astype(BF16), jnp.concatenate([vbuf[:hi, cols], ones[:hi]], axis=1))
            acc[lo:hi, cols] = o[:, :HD]
            l_out[lo:hi, cols] = o[:, HD:]


def frames_kernel(counts_ref, mask_ref, p1, p3, p2, x13, x2, c13, c2, q, w, acc_in, l_in, acc, l, x, kbuf, vbuf):
    width = q.shape[1]
    part = kbuf.shape[0]
    n = jnp.int32(0)
    groups = {
        1: (p1[...], x13[0], c13[0], c13[2]),
        2: (p2[...], x2[...], c2[0], c2[1]),
        3: (p3[...], x13[1], c13[1], c13[3]),
    }
    for d in range(1, REACH):
        nf = key_block(counts_ref, mask_ref, d, 0)
        for pay in groups[d]:
            x[pl.ds(pl.multiple_of(n * FT, FT), FT), :] = pay[:FT]
            n = n + (slot_of(pay) < nf).astype(jnp.int32)
    for j in range(part // FT):
        x[pl.ds(pl.multiple_of((n + j) * FT, FT), FT), :] = jnp.zeros((FT, x.shape[1]), BF16)

    def step(c, _):
        rows = x[pl.ds(pl.multiple_of(c * part, part), part), :]
        kbuf[...] = dot_nn(rows, w[1]).astype(BF16)
        vbuf[...] = dot_nn(rows, w[2]).astype(BF16)
        row = lax.broadcasted_iota(jnp.int32, (part, HD), 0)
        ones = jnp.where(row < n * FT - c * part, 1.0, 0.0).astype(BF16)
        for h in range(width // HD):
            cols = slice(h * HD, (h + 1) * HD)
            p = jnp.exp2(dot_nt(q[:, cols], kbuf[:, cols]) * SCALE).astype(BF16)
            o = dot_nn(p, jnp.concatenate([vbuf[:, cols], ones], axis=1))
            acc[:, cols] += o[:, :HD]
            l[:, cols] += o[:, HD:]
        return 0

    lax.fori_loop(0, (n * FT + part - 1) // part, step, 0)


def text_kernel(counts_ref, mask_ref, t1, t2, t3, q, acc, l, out, bad):
    span, width = q.shape
    cap = t1.shape[1]
    b = lax.axis_index("blk")
    row = lax.broadcasted_iota(jnp.int32, (cap, HD), 0)
    ones = jnp.concatenate(
        [jnp.where(row < key_block(counts_ref, mask_ref, d, 1), 1.0, 0.0).astype(BF16) for d in range(1, REACH)], axis=0
    )
    live = live_rows((span, HD), counts_ref[0, b], counts_ref[1, b], span - cap)
    worst = jnp.zeros((span, HD), F32)
    for h in range(width // HD):
        cols = slice(h * HD, (h + 1) * HD)
        keys = jnp.concatenate([t[0, :, cols] for t in (t1, t2, t3)], axis=0)
        values = jnp.concatenate([t[1, :, cols] for t in (t1, t2, t3)], axis=0) * ones
        p = jnp.exp2(dot_nt(q[:, cols], keys) * SCALE).astype(BF16)
        o = dot_nn(p, jnp.concatenate([values, ones], axis=1))
        s = l[:, cols] + o[:, HD:]
        worst = jnp.where((s > LOW) & (s < HIGH), worst, 1.0)
        out[:, cols] = jnp.where(live, (acc[:, cols] + o[:, :HD]) / s, 0.0).astype(BF16)
    bad[...] = jnp.max(jnp.where(live, worst, 0.0), axis=0, keepdims=True)


def exact_kernel(
    counts_ref, mask_ref, pay0, payx, payc, p1, p3, p2, x13, x2, c13, c2, tkv, t1, t2, t3, q, w, out,
    x, text, kbuf, vbuf, acc, m_all, l_all
):
    span, width = q.shape
    cap = tkv.shape[1]
    frames = span - cap
    b = lax.axis_index("blk")
    groups = (
        (pay0[...], payx[...], payc[0], payc[1]),
        (p1[...], x13[0], c13[0], c13[2]),
        (p2[...], x2[...], c2[0], c2[1]),
        (p3[...], x13[1], c13[1], c13[3]),
    )
    for d, texts in enumerate((tkv, t1, t2, t3)):
        for pay in groups[d]:
            x[pl.ds(pl.multiple_of(d * frames + slot_of(pay) * FT, FT), FT), :] = pay[:FT]
        text[d] = texts[...]
    acc[...] = jnp.zeros_like(acc)
    m_all[...] = jnp.full_like(m_all, NEG)
    l_all[...] = jnp.zeros_like(l_all)
    lane = lax.broadcasted_iota(jnp.int32, (span, HD), 1)
    qpos = lax.broadcasted_iota(jnp.int32, (span, span), 0)
    kpos = lax.broadcasted_iota(jnp.int32, (span, span), 1)

    def block(d, _):
        nf = counts_ref[0, jnp.maximum(b - d, 0)]
        nt = counts_ref[1, jnp.maximum(b - d, 0)]

        @pl.when(mask_ref[0, d] > 0)
        def _():
            rows = x[pl.ds(pl.multiple_of(d * frames, frames), frames), :]
            kbuf[:frames, :] = dot_nn(rows, w[1]).astype(BF16)
            vbuf[:frames, :] = dot_nn(rows, w[2]).astype(BF16)
            kbuf[frames:, :] = text[d, 0]
            vbuf[frames:, :] = text[d, 1]
            allowed = (kpos < nf * FT) | ((kpos >= frames) & (kpos - frames < nt))
            allowed = allowed & ((qpos >= kpos) | (jnp.zeros_like(kpos) + d > 0))
            bias = jnp.where(allowed, 0.0, NEG)

            def head(h, _):
                cols = pl.ds(pl.multiple_of(h * HD, HD), HD)
                old = jnp.max(jnp.where(lane == h, m_all[...], NEG), axis=1, keepdims=True)
                s = dot_nt(q[:, cols], kbuf[:, cols]) * SCALE + bias
                top = jnp.maximum(jnp.max(s, axis=1, keepdims=True), old)
                p = jnp.exp2(s - top)
                keep = jnp.exp2(old - top)
                acc[:, cols] = acc[:, cols] * keep + dot_nn(p.astype(BF16), vbuf[:, cols])
                total = jnp.sum(p, axis=1, keepdims=True)
                l_all[...] = jnp.where(lane == h, l_all[...] * keep + total, l_all[...])
                m_all[...] = jnp.where(lane == h, top, m_all[...])
                return 0

            lax.fori_loop(0, width // HD, head, 0)

        return 0

    lax.fori_loop(0, REACH, block, 0)
    live = live_rows((span, HD), counts_ref[0, b], counts_ref[1, b], frames)

    def finish(h, _):
        cols = pl.ds(pl.multiple_of(h * HD, HD), HD)
        total = jnp.max(jnp.where(lane == h, l_all[...], 0.0), axis=1, keepdims=True)
        out[:, cols] = jnp.where(live, acc[:, cols] / total, 0.0).astype(BF16)
        return 0

    lax.fori_loop(0, width // HD, finish, 0)


def shift(value, by):
    length = lax.axis_size("blk")
    return lax.ppermute(value, "blk", [(i, (i + by) % length) for i in range(length)])


def across(value, bit):
    return lax.ppermute(value, "tp", [(i, i ^ bit) for i in range(lax.axis_size("tp"))])


def after(value, *others):
    return lax.optimization_barrier((value, *others))


def body(text_query, text_keyval, frame_features, frame_proj, frame_slot, counts, block_mask):
    cap, width = text_query.shape
    frames = frame_slot.shape[1] * FT
    span = frames + cap
    vw = frame_features.shape[1]
    weights = jnp.transpose(frame_proj, (1, 0, 2))
    counts = counts.T
    pay = pl.pallas_call(
        prep_kernel,
        out_shape=jax.ShapeDtypeStruct((ROWS, vw), BF16),
        in_specs=[SM, VM],
        out_specs=VM,
        compiler_params=PARAMS,
        name="prep",
    )(frame_slot, frame_features)
    p3 = shift(pay, 3)
    p1 = shift(pay, 1)
    own_x = across(pay, 2)
    p1, p3, own_x, kv = after(p1, p3, own_x, text_keyval)
    own_c = across(jnp.stack([pay, own_x]), 1)
    pair = jnp.stack([p1, p3])
    x13 = across(pair, 2)
    p2 = shift(p3, -1)
    t3 = shift(kv, 3)
    t1 = shift(kv, 1)
    sums = jax.ShapeDtypeStruct((span, width), F32)
    q, acc, l = pl.pallas_call(
        own_kernel,
        out_shape=(jax.ShapeDtypeStruct((span, width), BF16), sums, sums),
        in_specs=[SM] + [VM] * 6,
        out_specs=(VM,) * 3,
        scratch_shapes=[
            pltpu.VMEM((frames, vw), BF16),
            pltpu.VMEM((span, width), BF16),
            pltpu.VMEM((span, width), BF16),
        ],
        compiler_params=PARAMS,
        name="own",
    )(counts, pay, own_x, own_c, text_query, text_keyval, weights)
    acc, p2, x13, t3 = after(acc, p2, x13, t3)
    x2 = across(p2, 2)
    c13 = across(jnp.concatenate([pair, x13]), 1)
    c2 = across(jnp.stack([p2, x2]), 1)
    t2 = shift(t3, -1)
    acc, l = pl.pallas_call(
        frames_kernel,
        out_shape=(sums, sums),
        in_specs=[SM, SM] + [VM] * 11,
        out_specs=(VM,) * 2,
        input_output_aliases={11: 0, 12: 1},
        scratch_shapes=[
            pltpu.VMEM((4 * frames, vw), BF16),
            pltpu.VMEM((frames, width), BF16),
            pltpu.VMEM((frames, width), BF16),
        ],
        compiler_params=PARAMS,
        name="frames",
    )(counts, block_mask, p1, p3, p2, x13, x2, c13, c2, q, weights, acc, l)
    out, bad = pl.pallas_call(
        text_kernel,
        out_shape=(jax.ShapeDtypeStruct((span, width), BF16), jax.ShapeDtypeStruct((1, HD), F32)),
        in_specs=[SM, SM] + [VM] * 6,
        out_specs=(VM, VM),
        compiler_params=PARAMS,
        name="text",
    )(counts, block_mask, t1, t2, t3, q, acc, l)

    def exact():
        return pl.pallas_call(
            exact_kernel,
            out_shape=jax.ShapeDtypeStruct((span, width), BF16),
            in_specs=[SM, SM] + [VM] * 16,
            out_specs=VM,
            scratch_shapes=[
                pltpu.VMEM((REACH * frames, vw), BF16),
                pltpu.VMEM((REACH, 2, cap, width), BF16),
                pltpu.VMEM((span, width), BF16),
                pltpu.VMEM((span, width), BF16),
                pltpu.VMEM((span, width), F32),
                pltpu.VMEM((span, HD), F32),
                pltpu.VMEM((span, HD), F32),
            ],
            compiler_params=pltpu.CompilerParams(vmem_limit_bytes=48 << 20),
            name="exact",
        )(
            counts, block_mask, pay, own_x, own_c, p1, p3, p2, x13, x2, c13, c2,
            text_keyval, t1, t2, t3, q, weights
        )

    return lax.cond(jnp.max(bad) > 0, exact, lambda: out)


def solution(mesh):
    placed = (
        P("blk", "tp"),
        P(None, "blk", "tp"),
        P(("blk", "tp"), None),
        P(None, None, "tp"),
        P("blk", None),
        P(),
        P("blk", None),
    )
    return jax.shard_map(
        body, mesh=mesh, in_specs=placed, out_specs=P("blk", "tp"), check_vma=False
    )
```

```python
import math

import jax
import jax.numpy as jnp
from jax import lax
from jax.experimental import pallas as pl
from jax.experimental.pallas import tpu as pltpu
from jax.sharding import PartitionSpec as P

HD = 128
FT = 64
REACH = 4
PAD = 8
ROWS = FT + PAD
NEG = -1e30
SCALE = 1.4426950408889634 / math.sqrt(HD)
LOW, HIGH = 2.0**-60, 2.0**100
VM = pl.BlockSpec(memory_space=pltpu.VMEM)
SM = pl.BlockSpec(memory_space=pltpu.SMEM)
HBM = pl.BlockSpec(memory_space=pltpu.HBM)
ANY = pl.BlockSpec(memory_space=pl.ANY)
F32 = jnp.float32
BF16 = jnp.bfloat16


def limit(mib):
    return pltpu.CompilerParams(vmem_limit_bytes=mib << 20)


def dot_nt(a, b):
    return lax.dot_general(a, b, (((1,), (1,)), ((), ())), preferred_element_type=F32)


def dot_nn(a, b):
    return lax.dot_general(a, b, (((1,), (0,)), ((), ())), preferred_element_type=F32)


def prep_kernel(slot_ref, feat_hbm, out_ref, feat_ref, sem):
    copy = pltpu.make_async_copy(feat_hbm, feat_ref, sem)
    copy.start()
    me = lax.axis_index("tp")
    slot = jnp.int32(0)
    for j in range(1, slot_ref.shape[1]):
        slot = jnp.where(slot_ref[0, j] == me, jnp.int32(j), slot)
    copy.wait()
    feats = feat_ref[...].astype(F32)
    normed = feats * lax.rsqrt(jnp.mean(feats * feats, axis=1, keepdims=True) + 1e-05)
    out_ref[:FT, :] = normed.astype(BF16)
    out_ref[FT:, :] = jnp.full((PAD, out_ref.shape[1]), slot.astype(F32), F32).astype(BF16)


def slot_of(pay):
    return jnp.max(pay[FT:ROWS, :128].astype(F32)).astype(jnp.int32)


def live_rows(shape, nf, nt, frames):
    row = lax.broadcasted_iota(jnp.int32, shape, 0)
    return (row < nf * FT) | ((row >= frames) & (row - frames < nt))


def key_block(counts_ref, mask_ref, d, which):
    b = lax.axis_index("blk")
    return jnp.where(mask_ref[0, d] > 0, counts_ref[which, jnp.maximum(b - d, 0)], 0)


def load_kernel(w_hbm, w, sems):
    n = w.shape[0]
    copies = [pltpu.make_async_copy(w_hbm.at[m], w.at[m], sems.at[m]) for m in range(n)]
    for copy in copies:
        copy.start()
    for copy in copies:
        copy.wait()


def own_kernel(counts_ref, pay0, payx, payc, tq, tkv, w, q_out, acc, l_out, x, kbuf, vbuf, sems):
    cap, width = tq.shape
    frames = x.shape[0]
    span = frames + cap
    half = width // 2
    copies = []
    for source, target in ((tq, q_out), (tkv.at[0], kbuf), (tkv.at[1], vbuf)):
        copies.append(pltpu.make_async_copy(source, target.at[pl.ds(frames, cap)], sems.at[len(copies)]))
        copies[-1].start()
    b = lax.axis_index("blk")
    nf = counts_ref[0, b]
    nt = counts_ref[1, b]
    for pay in (pay0[...], payx[...], payc[0], payc[1]):
        x[pl.ds(pl.multiple_of(slot_of(pay) * FT, FT), FT), :] = pay[:FT]
    rows = x[...]
    frow = lax.broadcasted_iota(jnp.int32, (frames, half), 0)
    for n in range(2):
        c = slice(n * half, (n + 1) * half)
        q_out[:frames, c] = dot_nn(rows, w[0, :, c]).astype(BF16)
        kbuf[:frames, c] = dot_nn(rows, w[1, :, c]).astype(BF16)
        vbuf[:frames, c] = jnp.where(frow < nf * FT, dot_nn(rows, w[2, :, c]), 0.0).astype(BF16)
    for copy in copies:
        copy.wait()
    trow = lax.broadcasted_iota(jnp.int32, (cap, width), 0)
    texts = vbuf[frames:, :]
    vbuf[frames:, :] = jnp.where(trow < nt, texts, jnp.zeros_like(texts))
    ones = jnp.where(live_rows((span, HD), nf, nt, frames), 1.0, 0.0).astype(BF16)
    step = cap
    causal = lax.broadcasted_iota(jnp.int32, (step, step), 0) >= lax.broadcasted_iota(jnp.int32, (step, step), 1)
    for h in range(width // HD):
        cols = slice(h * HD, (h + 1) * HD)
        for lo in range(0, span, step):
            hi = lo + step
            p = jnp.exp2(dot_nt(q_out[lo:hi, cols], kbuf[:hi, cols]) * SCALE)
            diag = jnp.where(causal, p[:, lo:hi], 0.0)
            p = jnp.concatenate([p[:, :lo], diag], axis=1) if lo else diag
            o = dot_nn(p.astype(BF16), jnp.concatenate([vbuf[:hi, cols], ones[:hi]], axis=1))
            acc[lo:hi, cols] = o[:, :HD]
            l_out[lo:hi, cols] = o[:, HD:]


def frames_kernel(counts_ref, mask_ref, pair, gx, gc, q, w, acc_in, l_in, acc, l, x, kbuf, vbuf):
    width = q.shape[1]
    part = kbuf.shape[0]
    n = jnp.int32(0)
    groups = {
        d: (pair[d - 1], gx[d - 1], gc[d - 1], gc[d + 2]) for d in range(1, REACH)
    }
    for d in range(1, REACH):
        nf = key_block(counts_ref, mask_ref, d, 0)
        for pay in groups[d]:
            x[pl.ds(pl.multiple_of(n * FT, FT), FT), :] = pay[:FT]
            n = n + (slot_of(pay) < nf).astype(jnp.int32)
    for j in range(part // FT):
        x[pl.ds(pl.multiple_of((n + j) * FT, FT), FT), :] = jnp.zeros((FT, x.shape[1]), BF16)

    def step(c, _):
        rows = x[pl.ds(pl.multiple_of(c * part, part), part), :]
        kbuf[...] = dot_nn(rows, w[1]).astype(BF16)
        vbuf[...] = dot_nn(rows, w[2]).astype(BF16)
        row = lax.broadcasted_iota(jnp.int32, (part, HD), 0)
        ones = jnp.where(row < n * FT - c * part, 1.0, 0.0).astype(BF16)
        for h in range(width // HD):
            cols = slice(h * HD, (h + 1) * HD)
            p = jnp.exp2(dot_nt(q[:, cols], kbuf[:, cols]) * SCALE).astype(BF16)
            o = dot_nn(p, jnp.concatenate([vbuf[:, cols], ones], axis=1))
            acc[:, cols] += o[:, :HD]
            l[:, cols] += o[:, HD:]
        return 0

    lax.fori_loop(0, (n * FT + part - 1) // part, step, 0)


def text_kernel(
    counts_ref, mask_ref, t1, t2, t3, q, acc, l, pay0, payx, payc, trio, gx, gc, tkv, w, out,
    sem, pay, wbuf, x, text, kbuf, vbuf, esum, m_all, l_all
):
    span, width = q.shape
    cap = t1.shape[1]
    b = lax.axis_index("blk")
    row = lax.broadcasted_iota(jnp.int32, (cap, HD), 0)
    ones = jnp.concatenate(
        [jnp.where(row < key_block(counts_ref, mask_ref, d, 1), 1.0, 0.0).astype(BF16) for d in range(1, REACH)], axis=0
    )
    live = live_rows((span, HD), counts_ref[0, b], counts_ref[1, b], span - cap)
    worst = jnp.zeros((span, HD), F32)
    for h in range(width // HD):
        cols = slice(h * HD, (h + 1) * HD)
        keys = jnp.concatenate([t[0, :, cols] for t in (t1, t2, t3)], axis=0)
        values = jnp.concatenate([t[1, :, cols] for t in (t1, t2, t3)], axis=0) * ones
        p = jnp.exp2(dot_nt(q[:, cols], keys) * SCALE).astype(BF16)
        o = dot_nn(p, jnp.concatenate([values, ones], axis=1))
        s = l[:, cols] + o[:, HD:]
        worst = jnp.where((s > LOW) & (s < HIGH), worst, 1.0)
        out[:, cols] = jnp.where(live, (acc[:, cols] + o[:, :HD]) / s, 0.0).astype(BF16)
    bad = jnp.max(jnp.where(live, worst, 0.0))

    @pl.when(bad > 0)
    def _():
        exact(
            counts_ref, mask_ref, (tkv, t1, t2, t3), q, (pay0, payx, payc, trio, gx, gc), w, out,
            sem, pay, wbuf, x, text, kbuf, vbuf, esum, m_all, l_all
        )


def fetch(source, target, sem):
    copy = pltpu.make_async_copy(source, target, sem)
    copy.start()
    copy.wait()


def exact(
    counts_ref, mask_ref, texts, q, pays, w, out, sem, pay, wbuf, x, text, kbuf, vbuf, acc, m_all, l_all
):
    span, width = q.shape
    cap = text.shape[2]
    frames = span - cap
    b = lax.axis_index("blk")
    pay0, payx, payc, trio, gx, gc = pays
    fetch(w.at[pl.ds(1, 2)], wbuf, sem)
    for d in range(REACH):
        if d:
            group = (trio.at[d - 1], gx.at[d - 1], gc.at[d - 1], gc.at[d + 2])
        else:
            group = (pay0, payx, payc.at[0], payc.at[1])
        for one in group:
            fetch(one, pay, sem)
            x[pl.ds(pl.multiple_of(d * frames + slot_of(pay) * FT, FT), FT), :] = pay[:FT]
        fetch(texts[d], text.at[d], sem)
    acc[...] = jnp.zeros_like(acc)
    m_all[...] = jnp.full_like(m_all, NEG)
    l_all[...] = jnp.zeros_like(l_all)
    lane = lax.broadcasted_iota(jnp.int32, (span, HD), 1)
    qpos = lax.broadcasted_iota(jnp.int32, (span, span), 0)
    kpos = lax.broadcasted_iota(jnp.int32, (span, span), 1)

    def block(d, _):
        nf = counts_ref[0, jnp.maximum(b - d, 0)]
        nt = counts_ref[1, jnp.maximum(b - d, 0)]

        @pl.when(mask_ref[0, d] > 0)
        def _():
            rows = x[pl.ds(pl.multiple_of(d * frames, frames), frames), :]
            kbuf[:frames, :] = dot_nn(rows, wbuf[0]).astype(BF16)
            vbuf[:frames, :] = dot_nn(rows, wbuf[1]).astype(BF16)
            kbuf[frames:, :] = text[d, 0]
            vbuf[frames:, :] = text[d, 1]
            allowed = (kpos < nf * FT) | ((kpos >= frames) & (kpos - frames < nt))
            allowed = allowed & ((qpos >= kpos) | (jnp.zeros_like(kpos) + d > 0))
            bias = jnp.where(allowed, 0.0, NEG)

            def head(h, _):
                cols = pl.ds(pl.multiple_of(h * HD, HD), HD)
                old = jnp.max(jnp.where(lane == h, m_all[...], NEG), axis=1, keepdims=True)
                s = dot_nt(q[:, cols], kbuf[:, cols]) * SCALE + bias
                top = jnp.maximum(jnp.max(s, axis=1, keepdims=True), old)
                p = jnp.exp2(s - top)
                keep = jnp.exp2(old - top)
                acc[:, cols] = acc[:, cols] * keep + dot_nn(p.astype(BF16), vbuf[:, cols])
                total = jnp.sum(p, axis=1, keepdims=True)
                l_all[...] = jnp.where(lane == h, l_all[...] * keep + total, l_all[...])
                m_all[...] = jnp.where(lane == h, top, m_all[...])
                return 0

            lax.fori_loop(0, width // HD, head, 0)

        return 0

    lax.fori_loop(0, REACH, block, 0)
    live = live_rows((span, HD), counts_ref[0, b], counts_ref[1, b], frames)

    def finish(h, _):
        cols = pl.ds(pl.multiple_of(h * HD, HD), HD)
        total = jnp.max(jnp.where(lane == h, l_all[...], 0.0), axis=1, keepdims=True)
        out[:, cols] = jnp.where(live, acc[:, cols] / total, 0.0).astype(BF16)
        return 0

    lax.fori_loop(0, width // HD, finish, 0)


def leaves(i, length):
    return i % (length // 2) > length // 2 - REACH


def shift(value, by):
    length, tps = lax.axis_size("blk"), lax.axis_size("tp")
    pairs = []
    for i in range(length):
        j = (i + by) % length
        swap = 0 if j // (length // 2) == i // (length // 2) else 2
        pairs += [(i * tps + t, j * tps + (t ^ swap)) for t in range(tps)]
    return lax.ppermute(value, ("blk", "tp"), pairs)


def pass_heads(value, by, change):
    length, tps = lax.axis_size("blk"), lax.axis_size("tp")
    pairs = []
    for i in range(length):
        swap = 2 if change and leaves(i, length) else 0
        pairs += [(i * tps + t, (i + by) % length * tps + (t ^ swap)) for t in range(tps)]
    return lax.ppermute(value, ("blk", "tp"), pairs)


def across(value, bit):
    return lax.ppermute(value, "tp", [(i, i ^ bit) for i in range(lax.axis_size("tp"))])


def stay(value):
    return pltpu.with_memory_space_constraint(value, pltpu.HBM)


def after(value, *others):
    return lax.optimization_barrier((value, *others))


def body(text_query, text_keyval, frame_features, frame_proj, frame_slot, counts, block_mask):
    cap, width = text_query.shape
    frames = frame_slot.shape[1] * FT
    span = frames + cap
    vw = frame_features.shape[1]
    weights = stay(jnp.transpose(frame_proj, (1, 0, 2)))
    counts, frame_slot, block_mask = stay(counts.T), stay(frame_slot), stay(block_mask)
    frame_features, text_query, text_kv = stay(frame_features), stay(text_query), stay(text_keyval)
    pay = pl.pallas_call(
        prep_kernel,
        out_shape=jax.ShapeDtypeStruct((ROWS, vw), BF16),
        in_specs=[SM, HBM],
        out_specs=VM,
        scratch_shapes=[pltpu.VMEM((FT, vw), BF16), pltpu.SemaphoreType.DMA],
        compiler_params=limit(4),
        name="prep",
    )(frame_slot, frame_features)
    w = pl.pallas_call(
        load_kernel,
        out_shape=pltpu.VMEM(weights.shape, BF16),
        in_specs=[HBM],
        out_specs=VM,
        scratch_shapes=[pltpu.SemaphoreType.DMA((weights.shape[0],))],
        compiler_params=limit(2),
        name="load",
    )(weights)
    p2 = shift(pay, 2)
    p3 = shift(pay, 3)
    p1 = shift(pay, 1)
    own_x = across(pay, 2)
    sent = pass_heads(text_keyval, 0, True)
    p1, p2, p3, own_x, sent, w = after(p1, p2, p3, own_x, sent, w)
    own_c = across(jnp.stack([pay, own_x]), 1)
    trio = jnp.stack([p1, p2, p3])
    gx = across(trio, 2)
    t3 = pass_heads(sent, 3, True)
    sums = jax.ShapeDtypeStruct((span, width), F32)
    q, acc, l = pl.pallas_call(
        own_kernel,
        out_shape=(jax.ShapeDtypeStruct((span, width), BF16), sums, sums),
        in_specs=[SM] + [VM] * 3 + [HBM] * 2 + [VM],
        out_specs=(VM,) * 3,
        scratch_shapes=[
            pltpu.VMEM((frames, vw), BF16),
            pltpu.VMEM((span, width), BF16),
            pltpu.VMEM((span, width), BF16),
            pltpu.SemaphoreType.DMA((3,)),
        ],
        compiler_params=limit(12),
        name="own",
    )(counts, pay, own_x, own_c, text_query, text_kv, w)
    acc, gx = after(acc, gx)
    gc = across(jnp.concatenate([trio, gx]), 1)
    acc, t3 = after(acc, t3)
    t2 = pass_heads(t3, -1, False)
    t1 = pass_heads(sent, 1, True)
    acc, l = pl.pallas_call(
        frames_kernel,
        out_shape=(sums, sums),
        in_specs=[SM, SM] + [VM] * 7,
        out_specs=(VM,) * 2,
        input_output_aliases={7: 0, 8: 1},
        scratch_shapes=[
            pltpu.VMEM((4 * frames, vw), BF16),
            pltpu.VMEM((frames, width), BF16),
            pltpu.VMEM((frames, width), BF16),
        ],
        compiler_params=limit(12),
        name="frames",
    )(counts, block_mask, trio, gx, gc, q, w, acc, l)
    return pl.pallas_call(
        text_kernel,
        out_shape=jax.ShapeDtypeStruct((span, width), BF16),
        in_specs=[SM, SM] + [VM] * 6 + [ANY] * 8,
        out_specs=VM,
        scratch_shapes=[
            pltpu.SemaphoreType.DMA,
            pltpu.VMEM((ROWS, vw), BF16),
            pltpu.VMEM((2, vw, width), BF16),
            pltpu.VMEM((REACH * frames, vw), BF16),
            pltpu.VMEM((REACH, 2, cap, width), BF16),
            pltpu.VMEM((span, width), BF16),
            pltpu.VMEM((span, width), BF16),
            pltpu.VMEM((span, width), F32),
            pltpu.VMEM((span, HD), F32),
            pltpu.VMEM((span, HD), F32),
        ],
        compiler_params=limit(22),
        name="text",
    )(counts, block_mask, t1, t2, t3, q, acc, l, pay, own_x, own_c, trio, gx, gc, text_kv, weights)


def solution(mesh):
    placed = (
        P("blk", "tp"),
        P(None, "blk", "tp"),
        P(("blk", "tp"), None),
        P(None, None, "tp"),
        P("blk", None),
        P(),
        P("blk", None),
    )
    return jax.shard_map(
        body, mesh=mesh, in_specs=placed, out_specs=P("blk", "tp"), check_vma=False
    )
```

```python
import math

import jax
import jax.numpy as jnp
from jax import lax
from jax.experimental import pallas as pl
from jax.experimental.pallas import tpu as pltpu
from jax.sharding import PartitionSpec as P

HD = 128
FT = 64
REACH = 4
PAD = 8
ROWS = FT + PAD
NEG = -1e30
SCALE = 1.4426950408889634 / math.sqrt(HD)
LOW, HIGH = 2.0**-60, 2.0**100
VM = pl.BlockSpec(memory_space=pltpu.VMEM)
SM = pl.BlockSpec(memory_space=pltpu.SMEM)
HBM = pl.BlockSpec(memory_space=pltpu.HBM)
ANY = pl.BlockSpec(memory_space=pl.ANY)
F32 = jnp.float32
BF16 = jnp.bfloat16


def limit(mib):
    return pltpu.CompilerParams(vmem_limit_bytes=mib << 20)


def dot_nt(a, b):
    return lax.dot_general(a, b, (((1,), (1,)), ((), ())), preferred_element_type=F32)


def dot_nn(a, b):
    return lax.dot_general(a, b, (((1,), (0,)), ((), ())), preferred_element_type=F32)


def prep_kernel(slot_ref, feat_hbm, out_ref, feat_ref, sem):
    copy = pltpu.make_async_copy(feat_hbm, feat_ref, sem)
    copy.start()
    me = lax.axis_index("tp")
    slot = jnp.int32(0)
    for j in range(1, slot_ref.shape[1]):
        slot = jnp.where(slot_ref[0, j] == me, jnp.int32(j), slot)
    copy.wait()
    feats = feat_ref[...].astype(F32)
    normed = feats * lax.rsqrt(jnp.mean(feats * feats, axis=1, keepdims=True) + 1e-05)
    out_ref[:FT, :] = normed.astype(BF16)
    out_ref[FT:, :] = jnp.full((PAD, out_ref.shape[1]), slot.astype(F32), F32).astype(BF16)


def slot_of(pay):
    return jnp.max(pay[FT:ROWS, :128].astype(F32)).astype(jnp.int32)


def live_rows(shape, nf, nt, frames):
    row = lax.broadcasted_iota(jnp.int32, shape, 0)
    return (row < nf * FT) | ((row >= frames) & (row - frames < nt))


def key_block(counts_ref, mask_ref, d, which):
    b = lax.axis_index("blk")
    return jnp.where(mask_ref[0, d] > 0, counts_ref[which, jnp.maximum(b - d, 0)], 0)


def load_kernel(w_hbm, w, sems):
    n = w.shape[0]
    copies = [pltpu.make_async_copy(w_hbm.at[m], w.at[m], sems.at[m]) for m in range(n)]
    for copy in copies:
        copy.start()
    for copy in copies:
        copy.wait()


def own_kernel(counts_ref, pay0, payx, payc, tq, tkv, w, q_out, acc, l_out, x, kbuf, vbuf, sems):
    cap, width = tq.shape
    frames = x.shape[0]
    span = frames + cap
    half = width // 2
    copies = []
    for source, target in ((tq, q_out), (tkv.at[0], kbuf), (tkv.at[1], vbuf)):
        copies.append(pltpu.make_async_copy(source, target.at[pl.ds(frames, cap)], sems.at[len(copies)]))
        copies[-1].start()
    b = lax.axis_index("blk")
    nf = counts_ref[0, b]
    nt = counts_ref[1, b]
    for pay in (pay0[...], payx[...], payc[0], payc[1]):
        x[pl.ds(pl.multiple_of(slot_of(pay) * FT, FT), FT), :] = pay[:FT]
    rows = x[...]
    frow = lax.broadcasted_iota(jnp.int32, (frames, half), 0)
    for n in range(2):
        c = slice(n * half, (n + 1) * half)
        q_out[:frames, c] = dot_nn(rows, w[0, :, c]).astype(BF16)
        kbuf[:frames, c] = dot_nn(rows, w[1, :, c]).astype(BF16)
        vbuf[:frames, c] = jnp.where(frow < nf * FT, dot_nn(rows, w[2, :, c]), 0.0).astype(BF16)
    for copy in copies:
        copy.wait()
    trow = lax.broadcasted_iota(jnp.int32, (cap, width), 0)
    texts = vbuf[frames:, :]
    vbuf[frames:, :] = jnp.where(trow < nt, texts, jnp.zeros_like(texts))
    ones = jnp.where(live_rows((span, HD), nf, nt, frames), 1.0, 0.0).astype(BF16)
    step = cap
    causal = lax.broadcasted_iota(jnp.int32, (step, step), 0) >= lax.broadcasted_iota(jnp.int32, (step, step), 1)
    for h in range(width // HD):
        cols = slice(h * HD, (h + 1) * HD)
        for lo in range(0, span, step):
            hi = lo + step
            p = jnp.exp2(dot_nt(q_out[lo:hi, cols], kbuf[:hi, cols]) * SCALE)
            diag = jnp.where(causal, p[:, lo:hi], 0.0)
            p = jnp.concatenate([p[:, :lo], diag], axis=1) if lo else diag
            o = dot_nn(p.astype(BF16), jnp.concatenate([vbuf[:hi, cols], ones[:hi]], axis=1))
            acc[lo:hi, cols] = o[:, :HD]
            l_out[lo:hi, cols] = o[:, HD:]


def frames_kernel(counts_ref, mask_ref, pair, gx, gc, t3, q, w, acc_in, l_in, acc, l, x, kbuf, vbuf):
    width = q.shape[1]
    part = kbuf.shape[0]
    n = jnp.int32(0)
    groups = {
        d: (pair[d - 1], gx[d - 1], gc[d - 1], gc[d + 2]) for d in range(1, REACH)
    }
    for d in range(1, REACH):
        nf = key_block(counts_ref, mask_ref, d, 0)
        for pay in groups[d]:
            x[pl.ds(pl.multiple_of(n * FT, FT), FT), :] = pay[:FT]
            n = n + (slot_of(pay) < nf).astype(jnp.int32)
    for j in range(part // FT):
        x[pl.ds(pl.multiple_of((n + j) * FT, FT), FT), :] = jnp.zeros((FT, x.shape[1]), BF16)

    def step(c, _):
        rows = x[pl.ds(pl.multiple_of(c * part, part), part), :]
        kbuf[...] = dot_nn(rows, w[1]).astype(BF16)
        vbuf[...] = dot_nn(rows, w[2]).astype(BF16)
        row = lax.broadcasted_iota(jnp.int32, (part, HD), 0)
        ones = jnp.where(row < n * FT - c * part, 1.0, 0.0).astype(BF16)
        for h in range(width // HD):
            cols = slice(h * HD, (h + 1) * HD)
            p = jnp.exp2(dot_nt(q[:, cols], kbuf[:, cols]) * SCALE).astype(BF16)
            o = dot_nn(p, jnp.concatenate([vbuf[:, cols], ones], axis=1))
            acc[:, cols] += o[:, :HD]
            l[:, cols] += o[:, HD:]
        return 0

    lax.fori_loop(0, (n * FT + part - 1) // part, step, 0)
    live = key_block(counts_ref, mask_ref, REACH - 1, 1)

    @pl.when(live > 0)
    def _():
        ones = jnp.where(lax.broadcasted_iota(jnp.int32, (t3.shape[1], HD), 0) < live, 1.0, 0.0).astype(BF16)
        for h in range(width // HD):
            cols = slice(h * HD, (h + 1) * HD)
            p = jnp.exp2(dot_nt(q[:, cols], t3[0, :, cols]) * SCALE).astype(BF16)
            o = dot_nn(p, jnp.concatenate([t3[1, :, cols] * ones, ones], axis=1))
            acc[:, cols] += o[:, :HD]
            l[:, cols] += o[:, HD:]


def text_kernel(
    counts_ref, mask_ref, t1, t2, q, acc, l, t3, pay0, payx, payc, trio, gx, gc, tkv, w, out,
    sem, pay, wbuf, x, text, kbuf, vbuf, esum, m_all, l_all
):
    span, width = q.shape
    cap = t1.shape[1]
    b = lax.axis_index("blk")
    row = lax.broadcasted_iota(jnp.int32, (cap, HD), 0)
    ones = jnp.concatenate(
        [jnp.where(row < key_block(counts_ref, mask_ref, d, 1), 1.0, 0.0).astype(BF16) for d in (1, 2)], axis=0
    )
    live = live_rows((span, HD), counts_ref[0, b], counts_ref[1, b], span - cap)
    worst = jnp.zeros((span, HD), F32)
    for h in range(width // HD):
        cols = slice(h * HD, (h + 1) * HD)
        keys = jnp.concatenate([t[0, :, cols] for t in (t1, t2)], axis=0)
        values = jnp.concatenate([t[1, :, cols] for t in (t1, t2)], axis=0) * ones
        p = jnp.exp2(dot_nt(q[:, cols], keys) * SCALE).astype(BF16)
        o = dot_nn(p, jnp.concatenate([values, ones], axis=1))
        s = l[:, cols] + o[:, HD:]
        worst = jnp.where((s > LOW) & (s < HIGH), worst, 1.0)
        out[:, cols] = jnp.where(live, (acc[:, cols] + o[:, :HD]) / s, 0.0).astype(BF16)
    bad = jnp.max(jnp.where(live, worst, 0.0))

    @pl.when(bad > 0)
    def _():
        exact(
            counts_ref, mask_ref, (tkv, t1, t2, t3), q, (pay0, payx, payc, trio, gx, gc), w, out,
            sem, pay, wbuf, x, text, kbuf, vbuf, esum, m_all, l_all
        )


def fetch(source, target, sem):
    copy = pltpu.make_async_copy(source, target, sem)
    copy.start()
    copy.wait()


def exact(
    counts_ref, mask_ref, texts, q, pays, w, out, sem, pay, wbuf, x, text, kbuf, vbuf, acc, m_all, l_all
):
    span, width = q.shape
    cap = text.shape[2]
    frames = span - cap
    b = lax.axis_index("blk")
    pay0, payx, payc, trio, gx, gc = pays
    fetch(w.at[pl.ds(1, 2)], wbuf, sem)
    for d in range(REACH):
        if d:
            group = (trio.at[d - 1], gx.at[d - 1], gc.at[d - 1], gc.at[d + 2])
        else:
            group = (pay0, payx, payc.at[0], payc.at[1])
        for one in group:
            fetch(one, pay, sem)
            x[pl.ds(pl.multiple_of(d * frames + slot_of(pay) * FT, FT), FT), :] = pay[:FT]
        fetch(texts[d], text.at[d], sem)
    acc[...] = jnp.zeros_like(acc)
    m_all[...] = jnp.full_like(m_all, NEG)
    l_all[...] = jnp.zeros_like(l_all)
    lane = lax.broadcasted_iota(jnp.int32, (span, HD), 1)
    qpos = lax.broadcasted_iota(jnp.int32, (span, span), 0)
    kpos = lax.broadcasted_iota(jnp.int32, (span, span), 1)

    def block(d, _):
        nf = counts_ref[0, jnp.maximum(b - d, 0)]
        nt = counts_ref[1, jnp.maximum(b - d, 0)]

        @pl.when(mask_ref[0, d] > 0)
        def _():
            rows = x[pl.ds(pl.multiple_of(d * frames, frames), frames), :]
            kbuf[:frames, :] = dot_nn(rows, wbuf[0]).astype(BF16)
            vbuf[:frames, :] = dot_nn(rows, wbuf[1]).astype(BF16)
            kbuf[frames:, :] = text[d, 0]
            vbuf[frames:, :] = text[d, 1]
            allowed = (kpos < nf * FT) | ((kpos >= frames) & (kpos - frames < nt))
            allowed = allowed & ((qpos >= kpos) | (jnp.zeros_like(kpos) + d > 0))
            bias = jnp.where(allowed, 0.0, NEG)

            def head(h, _):
                cols = pl.ds(pl.multiple_of(h * HD, HD), HD)
                old = jnp.max(jnp.where(lane == h, m_all[...], NEG), axis=1, keepdims=True)
                s = dot_nt(q[:, cols], kbuf[:, cols]) * SCALE + bias
                top = jnp.maximum(jnp.max(s, axis=1, keepdims=True), old)
                p = jnp.exp2(s - top)
                keep = jnp.exp2(old - top)
                acc[:, cols] = acc[:, cols] * keep + dot_nn(p.astype(BF16), vbuf[:, cols])
                total = jnp.sum(p, axis=1, keepdims=True)
                l_all[...] = jnp.where(lane == h, l_all[...] * keep + total, l_all[...])
                m_all[...] = jnp.where(lane == h, top, m_all[...])
                return 0

            lax.fori_loop(0, width // HD, head, 0)

        return 0

    lax.fori_loop(0, REACH, block, 0)
    live = live_rows((span, HD), counts_ref[0, b], counts_ref[1, b], frames)

    def finish(h, _):
        cols = pl.ds(pl.multiple_of(h * HD, HD), HD)
        total = jnp.max(jnp.where(lane == h, l_all[...], 0.0), axis=1, keepdims=True)
        out[:, cols] = jnp.where(live, acc[:, cols] / total, 0.0).astype(BF16)
        return 0

    lax.fori_loop(0, width // HD, finish, 0)


def leaves(i, length):
    return i % (length // 2) > length // 2 - REACH


def shift(value, by):
    length, tps = lax.axis_size("blk"), lax.axis_size("tp")
    pairs = []
    for i in range(length):
        j = (i + by) % length
        swap = 0 if j // (length // 2) == i // (length // 2) else 2
        pairs += [(i * tps + t, j * tps + (t ^ swap)) for t in range(tps)]
    return lax.ppermute(value, ("blk", "tp"), pairs)


def pass_heads(value, by, change):
    length, tps = lax.axis_size("blk"), lax.axis_size("tp")
    pairs = []
    for i in range(length):
        swap = 2 if change and leaves(i, length) else 0
        pairs += [(i * tps + t, (i + by) % length * tps + (t ^ swap)) for t in range(tps)]
    return lax.ppermute(value, ("blk", "tp"), pairs)


def across(value, bit):
    return lax.ppermute(value, "tp", [(i, i ^ bit) for i in range(lax.axis_size("tp"))])


def stay(value):
    return pltpu.with_memory_space_constraint(value, pltpu.HBM)


def after(value, *others):
    return lax.optimization_barrier((value, *others))


def body(text_query, text_keyval, frame_features, frame_proj, frame_slot, counts, block_mask):
    cap, width = text_query.shape
    frames = frame_slot.shape[1] * FT
    span = frames + cap
    vw = frame_features.shape[1]
    weights = stay(jnp.transpose(frame_proj, (1, 0, 2)))
    counts, frame_slot, block_mask = stay(counts.T), stay(frame_slot), stay(block_mask)
    frame_features, text_query, text_kv = stay(frame_features), stay(text_query), stay(text_keyval)
    pay = pl.pallas_call(
        prep_kernel,
        out_shape=jax.ShapeDtypeStruct((ROWS, vw), BF16),
        in_specs=[SM, HBM],
        out_specs=VM,
        scratch_shapes=[pltpu.VMEM((FT, vw), BF16), pltpu.SemaphoreType.DMA],
        compiler_params=limit(4),
        name="prep",
    )(frame_slot, frame_features)
    w = pl.pallas_call(
        load_kernel,
        out_shape=pltpu.VMEM(weights.shape, BF16),
        in_specs=[HBM],
        out_specs=VM,
        scratch_shapes=[pltpu.SemaphoreType.DMA((weights.shape[0],))],
        compiler_params=limit(2),
        name="load",
    )(weights)
    p2 = shift(pay, 2)
    p3 = shift(pay, 3)
    p1 = shift(pay, 1)
    own_x = across(pay, 2)
    sent = pass_heads(text_keyval, 0, True)
    p1, p2, p3, sent, w = after(p1, p2, p3, sent, w)
    own_c = across(jnp.stack([pay, own_x]), 1)
    trio = jnp.stack([p1, p2, p3])
    gx = across(trio, 2)
    t3 = pass_heads(sent, 3, True)
    sums = jax.ShapeDtypeStruct((span, width), F32)
    q, acc, l = pl.pallas_call(
        own_kernel,
        out_shape=(jax.ShapeDtypeStruct((span, width), BF16), sums, sums),
        in_specs=[SM] + [VM] * 3 + [HBM] * 2 + [VM],
        out_specs=(VM,) * 3,
        scratch_shapes=[
            pltpu.VMEM((frames, vw), BF16),
            pltpu.VMEM((span, width), BF16),
            pltpu.VMEM((span, width), BF16),
            pltpu.SemaphoreType.DMA((3,)),
        ],
        compiler_params=limit(12),
        name="own",
    )(counts, pay, own_x, own_c, text_query, text_kv, w)
    acc, gx = after(acc, gx)
    gc = across(jnp.concatenate([trio, gx]), 1)
    acc, t3 = after(acc, t3)
    t2 = pass_heads(t3, -1, False)
    t1 = pass_heads(sent, 1, True)
    acc, l = pl.pallas_call(
        frames_kernel,
        out_shape=(sums, sums),
        in_specs=[SM, SM] + [VM] * 8,
        out_specs=(VM,) * 2,
        input_output_aliases={8: 0, 9: 1},
        scratch_shapes=[
            pltpu.VMEM((4 * frames, vw), BF16),
            pltpu.VMEM((frames, width), BF16),
            pltpu.VMEM((frames, width), BF16),
        ],
        compiler_params=limit(12),
        name="frames",
    )(counts, block_mask, trio, gx, gc, t3, q, w, acc, l)
    return pl.pallas_call(
        text_kernel,
        out_shape=jax.ShapeDtypeStruct((span, width), BF16),
        in_specs=[SM, SM] + [VM] * 5 + [ANY] * 9,
        out_specs=VM,
        scratch_shapes=[
            pltpu.SemaphoreType.DMA,
            pltpu.VMEM((ROWS, vw), BF16),
            pltpu.VMEM((2, vw, width), BF16),
            pltpu.VMEM((REACH * frames, vw), BF16),
            pltpu.VMEM((REACH, 2, cap, width), BF16),
            pltpu.VMEM((span, width), BF16),
            pltpu.VMEM((span, width), BF16),
            pltpu.VMEM((span, width), F32),
            pltpu.VMEM((span, HD), F32),
            pltpu.VMEM((span, HD), F32),
        ],
        compiler_params=limit(22),
        name="text",
    )(counts, block_mask, t1, t2, q, acc, l, t3, pay, own_x, own_c, trio, gx, gc, text_kv, weights)


def solution(mesh):
    placed = (
        P("blk", "tp"),
        P(None, "blk", "tp"),
        P(("blk", "tp"), None),
        P(None, None, "tp"),
        P("blk", None),
        P(),
        P("blk", None),
    )
    return jax.shard_map(
        body, mesh=mesh, in_specs=placed, out_specs=P("blk", "tp"), check_vma=False
    )
```

```python
import math

import jax
import jax.numpy as jnp
from jax import lax
from jax.experimental import pallas as pl
from jax.experimental.pallas import tpu as pltpu
from jax.sharding import PartitionSpec as P

HD = 128
FT = 64
REACH = 4
PAD = 8
ROWS = FT + PAD
NEG = -1e30
SCALE = 1.4426950408889634 / math.sqrt(HD)
LOW, HIGH = 2.0**-60, 2.0**100
VM = pl.BlockSpec(memory_space=pltpu.VMEM)
SM = pl.BlockSpec(memory_space=pltpu.SMEM)
HBM = pl.BlockSpec(memory_space=pltpu.HBM)
ANY = pl.BlockSpec(memory_space=pl.ANY)
F32 = jnp.float32
BF16 = jnp.bfloat16


def limit(mib):
    return pltpu.CompilerParams(vmem_limit_bytes=mib << 20)


def dot_nt(a, b):
    return lax.dot_general(a, b, (((1,), (1,)), ((), ())), preferred_element_type=F32)


def dot_nn(a, b):
    return lax.dot_general(a, b, (((1,), (0,)), ((), ())), preferred_element_type=F32)


def prep_kernel(slot_ref, feat_hbm, out_ref, feat_ref, sem):
    copy = pltpu.make_async_copy(feat_hbm, feat_ref, sem)
    copy.start()
    me = lax.axis_index("tp")
    slot = jnp.int32(0)
    for j in range(1, slot_ref.shape[1]):
        slot = jnp.where(slot_ref[0, j] == me, jnp.int32(j), slot)
    copy.wait()
    feats = feat_ref[...].astype(F32)
    normed = feats * lax.rsqrt(jnp.mean(feats * feats, axis=1, keepdims=True) + 1e-05)
    out_ref[:FT, :] = normed.astype(BF16)
    out_ref[FT:, :] = jnp.full((PAD, out_ref.shape[1]), slot.astype(F32), F32).astype(BF16)


def slot_of(pay):
    return jnp.max(pay[FT:ROWS, :128].astype(F32)).astype(jnp.int32)


def live_rows(shape, nf, nt, frames):
    row = lax.broadcasted_iota(jnp.int32, shape, 0)
    return (row < nf * FT) | ((row >= frames) & (row - frames < nt))


def key_block(counts_ref, mask_ref, d, which):
    b = lax.axis_index("blk")
    return jnp.where(mask_ref[0, d] > 0, counts_ref[which, jnp.maximum(b - d, 0)], 0)


def load_kernel(w_hbm, w, sems):
    n = w.shape[0]
    copies = [pltpu.make_async_copy(w_hbm.at[m], w.at[m], sems.at[m]) for m in range(n)]
    for copy in copies:
        copy.start()
    for copy in copies:
        copy.wait()


def own_kernel(counts_ref, pay0, payx, payc, tq, tkv, w, q_out, acc, l_out, x, kbuf, vbuf, sems):
    cap, width = tq.shape
    frames = x.shape[0]
    span = frames + cap
    half = width // 2
    copies = []
    for source, target in ((tq, q_out), (tkv.at[0], kbuf), (tkv.at[1], vbuf)):
        copies.append(pltpu.make_async_copy(source, target.at[pl.ds(frames, cap)], sems.at[len(copies)]))
        copies[-1].start()
    b = lax.axis_index("blk")
    nf = counts_ref[0, b]
    nt = counts_ref[1, b]
    for pay in (pay0[...], payx[...], payc[0], payc[1]):
        x[pl.ds(pl.multiple_of(slot_of(pay) * FT, FT), FT), :] = pay[:FT]
    rows = x[...]
    frow = lax.broadcasted_iota(jnp.int32, (frames, half), 0)
    for n in range(2):
        c = slice(n * half, (n + 1) * half)
        q_out[:frames, c] = dot_nn(rows, w[0, :, c]).astype(BF16)
        kbuf[:frames, c] = dot_nn(rows, w[1, :, c]).astype(BF16)
        vbuf[:frames, c] = jnp.where(frow < nf * FT, dot_nn(rows, w[2, :, c]), 0.0).astype(BF16)
    for copy in copies:
        copy.wait()
    trow = lax.broadcasted_iota(jnp.int32, (cap, width), 0)
    texts = vbuf[frames:, :]
    vbuf[frames:, :] = jnp.where(trow < nt, texts, jnp.zeros_like(texts))
    ones = jnp.where(live_rows((span, HD), nf, nt, frames), 1.0, 0.0).astype(BF16)
    step = cap
    causal = lax.broadcasted_iota(jnp.int32, (step, step), 0) >= lax.broadcasted_iota(jnp.int32, (step, step), 1)
    for h in range(width // HD):
        cols = slice(h * HD, (h + 1) * HD)
        for lo in range(0, span, step):
            hi = lo + step
            p = jnp.exp2(dot_nt(q_out[lo:hi, cols], kbuf[:hi, cols]) * SCALE)
            diag = jnp.where(causal, p[:, lo:hi], 0.0)
            p = jnp.concatenate([p[:, :lo], diag], axis=1) if lo else diag
            o = dot_nn(p.astype(BF16), jnp.concatenate([vbuf[:hi, cols], ones[:hi]], axis=1))
            acc[lo:hi, cols] = o[:, :HD]
            l_out[lo:hi, cols] = o[:, HD:]


def frames_kernel(counts_ref, mask_ref, pair, gx, gc, t3, q, w, acc_in, l_in, acc, l, x, kbuf, vbuf):
    width = q.shape[1]
    part = kbuf.shape[0]
    n = jnp.int32(0)
    groups = {
        d: (pair[d - 1], gx[d - 1], gc[d - 1], gc[d + 2]) for d in range(1, REACH)
    }
    for d in range(1, REACH):
        nf = key_block(counts_ref, mask_ref, d, 0)
        for pay in groups[d]:
            x[pl.ds(pl.multiple_of(n * FT, FT), FT), :] = pay[:FT]
            n = n + (slot_of(pay) < nf).astype(jnp.int32)
    for j in range(part // FT):
        x[pl.ds(pl.multiple_of((n + j) * FT, FT), FT), :] = jnp.zeros((FT, x.shape[1]), BF16)

    def step(c, _):
        rows = x[pl.ds(pl.multiple_of(c * part, part), part), :]
        kbuf[...] = dot_nn(rows, w[1]).astype(BF16)
        vbuf[...] = dot_nn(rows, w[2]).astype(BF16)
        row = lax.broadcasted_iota(jnp.int32, (part, HD), 0)
        ones = jnp.where(row < n * FT - c * part, 1.0, 0.0).astype(BF16)
        for h in range(width // HD):
            cols = slice(h * HD, (h + 1) * HD)
            p = jnp.exp2(dot_nt(q[:, cols], kbuf[:, cols]) * SCALE).astype(BF16)
            o = dot_nn(p, jnp.concatenate([vbuf[:, cols], ones], axis=1))
            acc[:, cols] += o[:, :HD]
            l[:, cols] += o[:, HD:]
        return 0

    lax.fori_loop(0, (n * FT + part - 1) // part, step, 0)
    live = key_block(counts_ref, mask_ref, REACH - 1, 1)

    @pl.when(live > 0)
    def _():
        ones = jnp.where(lax.broadcasted_iota(jnp.int32, (t3.shape[1], HD), 0) < live, 1.0, 0.0).astype(BF16)
        for h in range(width // HD):
            cols = slice(h * HD, (h + 1) * HD)
            p = jnp.exp2(dot_nt(q[:, cols], t3[0, :, cols]) * SCALE).astype(BF16)
            o = dot_nn(p, jnp.concatenate([t3[1, :, cols] * ones, ones], axis=1))
            acc[:, cols] += o[:, :HD]
            l[:, cols] += o[:, HD:]


def text_kernel(
    counts_ref, mask_ref, t1, t2, q, acc, l, t3, pay0, payx, payc, trio, gx, gc, tkv, w, out,
    flag, sem, pay, wbuf, x, text, kbuf, vbuf, esum, m_all, l_all
):
    span, width = q.shape
    cap = t1.shape[1]
    b = lax.axis_index("blk")
    row = lax.broadcasted_iota(jnp.int32, (cap, HD), 0)
    tokens = [key_block(counts_ref, mask_ref, d, 1) for d in (1, 2)]
    live = live_rows((span, HD), counts_ref[0, b], counts_ref[1, b], span - cap)

    def finish(chosen):
        if chosen:
            ones = jnp.concatenate([jnp.where(row < tokens[c], 1.0, 0.0).astype(BF16) for c in chosen], axis=0)
        worst = jnp.zeros((span, HD), F32)
        for h in range(width // HD):
            cols = slice(h * HD, (h + 1) * HD)
            a, s = acc[:, cols], l[:, cols]
            if chosen:
                keys = jnp.concatenate([(t1, t2)[c][0, :, cols] for c in chosen], axis=0)
                values = jnp.concatenate([(t1, t2)[c][1, :, cols] for c in chosen], axis=0) * ones
                p = jnp.exp2(dot_nt(q[:, cols], keys) * SCALE).astype(BF16)
                o = dot_nn(p, jnp.concatenate([values, ones], axis=1))
                a, s = a + o[:, :HD], s + o[:, HD:]
            worst = jnp.where((s > LOW) & (s < HIGH), worst, 1.0)
            out[:, cols] = jnp.where(live, a / s, 0.0).astype(BF16)
        flag[0] = jnp.max(jnp.where(live, worst, 0.0)).astype(jnp.int32)

    for chosen in ((0, 1), (0,), (1,), ()):
        use = jnp.bool_(True)
        for c in range(2):
            use = use & ((tokens[c] > 0) if c in chosen else (tokens[c] <= 0))
        pl.when(use)(lambda chosen=chosen: finish(chosen))
    bad = flag[0]

    @pl.when(bad > 0)
    def _():
        exact(
            counts_ref, mask_ref, (tkv, t1, t2, t3), q, (pay0, payx, payc, trio, gx, gc), w, out,
            sem, pay, wbuf, x, text, kbuf, vbuf, esum, m_all, l_all
        )


def fetch(source, target, sem):
    copy = pltpu.make_async_copy(source, target, sem)
    copy.start()
    copy.wait()


def exact(
    counts_ref, mask_ref, texts, q, pays, w, out, sem, pay, wbuf, x, text, kbuf, vbuf, acc, m_all, l_all
):
    span, width = q.shape
    cap = text.shape[2]
    frames = span - cap
    b = lax.axis_index("blk")
    pay0, payx, payc, trio, gx, gc = pays
    fetch(w.at[pl.ds(1, 2)], wbuf, sem)
    for d in range(REACH):
        if d:
            group = (trio.at[d - 1], gx.at[d - 1], gc.at[d - 1], gc.at[d + 2])
        else:
            group = (pay0, payx, payc.at[0], payc.at[1])
        for one in group:
            fetch(one, pay, sem)
            x[pl.ds(pl.multiple_of(d * frames + slot_of(pay) * FT, FT), FT), :] = pay[:FT]
        fetch(texts[d], text.at[d], sem)
    acc[...] = jnp.zeros_like(acc)
    m_all[...] = jnp.full_like(m_all, NEG)
    l_all[...] = jnp.zeros_like(l_all)
    lane = lax.broadcasted_iota(jnp.int32, (span, HD), 1)
    qpos = lax.broadcasted_iota(jnp.int32, (span, span), 0)
    kpos = lax.broadcasted_iota(jnp.int32, (span, span), 1)

    def block(d, _):
        nf = counts_ref[0, jnp.maximum(b - d, 0)]
        nt = counts_ref[1, jnp.maximum(b - d, 0)]

        @pl.when(mask_ref[0, d] > 0)
        def _():
            rows = x[pl.ds(pl.multiple_of(d * frames, frames), frames), :]
            kbuf[:frames, :] = dot_nn(rows, wbuf[0]).astype(BF16)
            vbuf[:frames, :] = dot_nn(rows, wbuf[1]).astype(BF16)
            kbuf[frames:, :] = text[d, 0]
            vbuf[frames:, :] = text[d, 1]
            allowed = (kpos < nf * FT) | ((kpos >= frames) & (kpos - frames < nt))
            allowed = allowed & ((qpos >= kpos) | (jnp.zeros_like(kpos) + d > 0))
            bias = jnp.where(allowed, 0.0, NEG)

            def head(h, _):
                cols = pl.ds(pl.multiple_of(h * HD, HD), HD)
                old = jnp.max(jnp.where(lane == h, m_all[...], NEG), axis=1, keepdims=True)
                s = dot_nt(q[:, cols], kbuf[:, cols]) * SCALE + bias
                top = jnp.maximum(jnp.max(s, axis=1, keepdims=True), old)
                p = jnp.exp2(s - top)
                keep = jnp.exp2(old - top)
                acc[:, cols] = acc[:, cols] * keep + dot_nn(p.astype(BF16), vbuf[:, cols])
                total = jnp.sum(p, axis=1, keepdims=True)
                l_all[...] = jnp.where(lane == h, l_all[...] * keep + total, l_all[...])
                m_all[...] = jnp.where(lane == h, top, m_all[...])
                return 0

            lax.fori_loop(0, width // HD, head, 0)

        return 0

    lax.fori_loop(0, REACH, block, 0)
    live = live_rows((span, HD), counts_ref[0, b], counts_ref[1, b], frames)

    def finish(h, _):
        cols = pl.ds(pl.multiple_of(h * HD, HD), HD)
        total = jnp.max(jnp.where(lane == h, l_all[...], 0.0), axis=1, keepdims=True)
        out[:, cols] = jnp.where(live, acc[:, cols] / total, 0.0).astype(BF16)
        return 0

    lax.fori_loop(0, width // HD, finish, 0)


def leaves(i, length):
    return i % (length // 2) > length // 2 - REACH


def shift(value, by):
    length, tps = lax.axis_size("blk"), lax.axis_size("tp")
    pairs = []
    for i in range(length):
        j = (i + by) % length
        swap = 0 if j // (length // 2) == i // (length // 2) else 2
        pairs += [(i * tps + t, j * tps + (t ^ swap)) for t in range(tps)]
    return lax.ppermute(value, ("blk", "tp"), pairs)


def pass_heads(value, by, change):
    length, tps = lax.axis_size("blk"), lax.axis_size("tp")
    pairs = []
    for i in range(length):
        swap = 2 if change and leaves(i, length) else 0
        pairs += [(i * tps + t, (i + by) % length * tps + (t ^ swap)) for t in range(tps)]
    return lax.ppermute(value, ("blk", "tp"), pairs)


def across(value, bit):
    return lax.ppermute(value, "tp", [(i, i ^ bit) for i in range(lax.axis_size("tp"))])


def stay(value):
    return pltpu.with_memory_space_constraint(value, pltpu.HBM)


def after(value, *others):
    return lax.optimization_barrier((value, *others))


def body(text_query, text_keyval, frame_features, frame_proj, frame_slot, counts, block_mask):
    cap, width = text_query.shape
    frames = frame_slot.shape[1] * FT
    span = frames + cap
    vw = frame_features.shape[1]
    weights = stay(jnp.transpose(frame_proj, (1, 0, 2)))
    counts, frame_slot, block_mask = stay(counts.T), stay(frame_slot), stay(block_mask)
    frame_features, text_query, text_kv = stay(frame_features), stay(text_query), stay(text_keyval)
    pay = pl.pallas_call(
        prep_kernel,
        out_shape=jax.ShapeDtypeStruct((ROWS, vw), BF16),
        in_specs=[SM, HBM],
        out_specs=VM,
        scratch_shapes=[pltpu.VMEM((FT, vw), BF16), pltpu.SemaphoreType.DMA],
        compiler_params=limit(4),
        name="prep",
    )(frame_slot, frame_features)
    w = pl.pallas_call(
        load_kernel,
        out_shape=pltpu.VMEM(weights.shape, BF16),
        in_specs=[HBM],
        out_specs=VM,
        scratch_shapes=[pltpu.SemaphoreType.DMA((weights.shape[0],))],
        compiler_params=limit(2),
        name="load",
    )(weights)
    p2 = shift(pay, 2)
    p3 = shift(pay, 3)
    p1 = shift(pay, 1)
    own_x = across(pay, 2)
    sent = pass_heads(text_keyval, 0, True)
    p1, p2, p3, sent, w = after(p1, p2, p3, sent, w)
    own_c = across(jnp.stack([pay, own_x]), 1)
    trio = jnp.stack([p1, p2, p3])
    gx = across(trio, 2)
    t3 = pass_heads(sent, 3, True)
    sums = jax.ShapeDtypeStruct((span, width), F32)
    q, acc, l = pl.pallas_call(
        own_kernel,
        out_shape=(jax.ShapeDtypeStruct((span, width), BF16), sums, sums),
        in_specs=[SM] + [VM] * 3 + [HBM] * 2 + [VM],
        out_specs=(VM,) * 3,
        scratch_shapes=[
            pltpu.VMEM((frames, vw), BF16),
            pltpu.VMEM((span, width), BF16),
            pltpu.VMEM((span, width), BF16),
            pltpu.SemaphoreType.DMA((3,)),
        ],
        compiler_params=limit(12),
        name="own",
    )(counts, pay, own_x, own_c, text_query, text_kv, w)
    acc, gx = after(acc, gx)
    gc = across(jnp.concatenate([trio, gx]), 1)
    acc, t3 = after(acc, t3)
    t2 = pass_heads(t3, -1, False)
    t1 = pass_heads(sent, 1, True)
    acc, l = pl.pallas_call(
        frames_kernel,
        out_shape=(sums, sums),
        in_specs=[SM, SM] + [VM] * 8,
        out_specs=(VM,) * 2,
        input_output_aliases={8: 0, 9: 1},
        scratch_shapes=[
            pltpu.VMEM((4 * frames, vw), BF16),
            pltpu.VMEM((frames, width), BF16),
            pltpu.VMEM((frames, width), BF16),
        ],
        compiler_params=limit(12),
        name="frames",
    )(counts, block_mask, trio, gx, gc, t3, q, w, acc, l)
    return pl.pallas_call(
        text_kernel,
        out_shape=jax.ShapeDtypeStruct((span, width), BF16),
        in_specs=[SM, SM] + [VM] * 5 + [ANY] * 9,
        out_specs=VM,
        scratch_shapes=[
            pltpu.SMEM((1,), jnp.int32),
            pltpu.SemaphoreType.DMA,
            pltpu.VMEM((ROWS, vw), BF16),
            pltpu.VMEM((2, vw, width), BF16),
            pltpu.VMEM((REACH * frames, vw), BF16),
            pltpu.VMEM((REACH, 2, cap, width), BF16),
            pltpu.VMEM((span, width), BF16),
            pltpu.VMEM((span, width), BF16),
            pltpu.VMEM((span, width), F32),
            pltpu.VMEM((span, HD), F32),
            pltpu.VMEM((span, HD), F32),
        ],
        compiler_params=limit(22),
        name="text",
    )(counts, block_mask, t1, t2, q, acc, l, t3, pay, own_x, own_c, trio, gx, gc, text_kv, weights)


def solution(mesh):
    placed = (
        P("blk", "tp"),
        P(None, "blk", "tp"),
        P(("blk", "tp"), None),
        P(None, None, "tp"),
        P("blk", None),
        P(),
        P("blk", None),
    )
    return jax.shard_map(
        body, mesh=mesh, in_specs=placed, out_specs=P("blk", "tp"), check_vma=False
    )
```
